32 devices in a mesh: gx: 8 (over z, core), gy: 4 (over y, x).
Axes of the slice: x: 2, y: 2, z: 4, core: 2. Of those that a mesh axis runs over, the one named last changes fastest.
Arguments:
- grad_pressure: float32 [64, 128, 1024], P('gx', 'gy'), may hold values from -6 to 6
- beta: float32 [3, 64, 128, 1024], P(None, 'gx', 'gy'), may hold values from 0.25 to 4
- tile_rows: int32 [8192], P(('gx', 'gy')), may hold values from 0 to 2047
- tile_owner: int32 [8192, 1], P(('gx', 'gy')), may hold values from 0 to 31; in each aligned block of 256 rows (0 to 255, 256 to 511, ...) at most 8 rows name the same one
- tile_slot: int32 [8192], P(('gx', 'gy')), may hold values from 0 to 255
- face_mask: int32 [8192, 128], P(('gx', 'gy')), may hold values 0 or 1
- heights: float32 [3, 8192, 128], P(None, ('gx', 'gy')), may hold values from -6 to 6
Outputs:
- grad_rhs: float32 [64, 128, 1024], P('gx', 'gy')
- grad_heights: float32 [3, 8192, 128], P(None, ('gx', 'gy'))
The draws below stay inside these ranges and needn't reach their ends.
Inputs may be any that keep to these rules, and one draw needn't show every extreme that they name: `tile_rows`: each entry indexes a row of 128 cells inside its own device's block. `tile_owner`: among the 256 tiles of one device no owner is named more than 8 times.
All inputs are finite; a program needn't handle non-finite values. No bound on the sum of `face_mask` on one device may be relied on, other than what follows from the above.
Results may differ from the reference program's by a relative error of at most 0.000025.
Values sent between devices are 32-bit elements; how exact they have to be, the bound alone decides.
A program may use at most 192 MiB of HBM per device.

```python
import math
import jax
import jax.numpy as jnp
import numpy as np

CX = 8
CY = 32
NZ = 1024
ITERS = 3
STEPS = 4
NT = 256
SLOTS = 256
CAP = 8
NX = 64
NY = 128
N_GX = 8
N_GY = 4


def place_ends(entries, own_key, low, top_value):
    spot = [jax.random.randint(jax.random.fold_in(own_key, axis), (), 0, length) for axis, length in enumerate(entries.shape)]
    main_axis = entries.shape.index(max(entries.shape))
    neighbour = spot[:main_axis] + [(spot[main_axis] + 1) % entries.shape[main_axis]] + spot[main_axis + 1:]
    return entries.at[tuple(spot)].set(low).at[tuple(neighbour)].set(top_value)


def levels(stream_key, dims, split, smallest, high):
    gain, own = 1.0, jax.random.fold_in(stream_key, 6)
    for axis_at, shards_of in split:
        draws = jnp.exp(jax.random.uniform(jax.random.fold_in(own, axis_at), (shards_of,), jnp.float32, smallest / len(split), high / len(split)))
        gain = gain * jnp.repeat(draws, dims[axis_at] // shards_of).reshape([-1 if axis == axis_at else 1 for axis in range(len(dims))])
    return gain


def deal_out(stream_key, own, number, rows, number_of, top, reach, lean):
    ranking = jax.random.permutation(stream_key, number_of)
    packed, usual = shares(number_of, rows * top, reach, lean, True), shares(number_of, rows * top, reach, lean, False)
    places = jnp.arange(number_of)

    def named(sizes, offset_by):
        used = int((sizes > 0).sum())
        fixed = max(1, used // 4)
        moved = fixed + (places - fixed + offset_by * (used - fixed)) % max(1, number_of - fixed)
        return jnp.zeros((number_of,), jnp.int32).at[ranking[jnp.where(places < fixed, places, moved)]].set(jnp.asarray(sizes, jnp.int32))

    sizes = jnp.where(number % 4 == 0, named(packed, number // 4), named(usual, number - number // 4 - 1))
    mixed = jax.random.permutation(jax.random.fold_in(own, 3), number_of)
    source_of, sink = mixed[0:number_of // 2 * 2:2], mixed[1:number_of // 2 * 2:2]
    slack = jnp.minimum(sizes[source_of] - 1, reach - sizes[sink]) // 2
    slack = jnp.where((source_of == ranking[0]) | (sink == ranking[0]) | (sizes[sink] == 0), 0, jnp.maximum(slack, 0))
    moved = jax.random.randint(jax.random.fold_in(own, 4), (number_of // 2,), 0, 1 << 20) % (slack + 1)
    sizes = sizes.at[source_of].add(-moved).at[sink].add(moved)
    items = jnp.searchsorted(jnp.cumsum(sizes), jnp.arange(rows * top), side="right").astype(jnp.int32)
    listing = items.reshape(top, rows).T
    listing = listing[jax.random.permutation(jax.random.fold_in(own, 1), rows)]
    offset_by = jax.random.randint(jax.random.fold_in(own, 2), (rows, 1), 0, top)
    return jnp.take_along_axis(listing, (jnp.arange(top)[None, :] + offset_by) % top, axis=1)


def shares(count, total, most, skew, full):
    weights = [(1 << 20) // math.isqrt(standing ** skew) + 1 for standing in range(1, count + 1)]
    largest = most if full else min(most, max(-(-total // count), total * weights[0] // sum(weights)))
    least = 1 if total - largest >= count - 1 else 0
    counts, surplus = [largest] + [least] * (count - 1), total - largest - least * (count - 1)
    while surplus > 0:
        movable = [i for i in range(1, count) if counts[i] < largest] or [i for i in range(1, count) if counts[i] < most]
        mass, budget = sum([weights[i] for i in movable]), surplus
        for i in movable:
            more = min(most - counts[i], max(1, budget * weights[i] // mass), surplus)
            counts[i] = counts[i] + more
            surplus = surplus - more
    return np.array(counts)


def scatter_about(key, extent, scale, reach, split=(), kind=jnp.bfloat16):
    result = jax.random.normal(key, extent, jnp.float32) * scale
    if len(split) > 0:
        result = levels(key, extent, split, -0.22, 0.18) * result
    return jnp.clip(result, min=-reach, max=reach).astype(kind)


def setup_inputs(seed: int = 0) -> dict:
    key_of = jax.random.split(jax.random.key(seed), 8)
    grad_pressure = scatter_about(key_of[0], (NX, NY, NZ), 1.0, 6.0, ((0, 8), (1, 4)), jnp.float32)
    beta = jnp.clip(jnp.exp(math.log(4.0) - 2.7725887 * jax.random.uniform(key_of[1], (3, NX, NY, NZ), jnp.float32) ** levels(key_of[1], (3, NX, NY, NZ), ((1, 8), (2, 4)), -0.2, 0.2)), 0.25, 4.0)
    tile_rows = place_ends(jax.random.randint(key_of[2], (N_GX * N_GY * NT,), 0, CX * CY * NZ // 128), jax.random.fold_in(key_of[2], 1), 0, (CX * CY * NZ // 128) - 1).astype(jnp.int32)
    tile_owner_keys = jax.random.split(jax.random.fold_in(key_of[3], 1), (N_GX * N_GY * NT) // NT)
    tile_owner_turns = jax.random.permutation(jax.random.fold_in(key_of[3], 3), (N_GX * N_GY * NT) // NT)
    tile_owner = jax.vmap(lambda own, number: deal_out(jax.random.fold_in(key_of[3], 2), own, number, NT, N_GX * N_GY, 1, CAP, 2))(tile_owner_keys, tile_owner_turns).reshape((N_GX * N_GY * NT, 1))
    tile_slot = place_ends(jax.random.randint(key_of[4], (N_GX * N_GY * NT,), 0, SLOTS), jax.random.fold_in(key_of[4], 1), 0, SLOTS - 1).astype(jnp.int32)
    face_mask = place_ends((jax.random.randint(key_of[5], (N_GX * N_GY * NT, 128), 0, 4) < 3).astype(jnp.int32), jax.random.fold_in(key_of[5], 1), 0, 1)
    heights = scatter_about(key_of[6], (3, N_GX * N_GY * SLOTS, 128), 1.0, 6.0, ((1, 32),), jnp.float32)
    return {"grad_pressure": grad_pressure, "beta": beta, "tile_rows": tile_rows, "tile_owner": tile_owner, "tile_slot": tile_slot, "face_mask": face_mask, "heights": heights}


LOW_BOUND = 0.1
HIGH_BOUND = 1.9


def omega_of(step_index):
    theta = 0.5 * (HIGH_BOUND + LOW_BOUND) + 0.5 * (HIGH_BOUND - LOW_BOUND) * math.cos(math.pi * (2 * step_index + 1) / (2 * STEPS))
    return 1.0 / theta


def shifted_low(field, axis_number):
    first = jnp.zeros_like(jnp.take(field, jnp.arange(1), axis=axis_number))
    rest = jnp.take(field, jnp.arange(field.shape[axis_number] - 1), axis=axis_number)
    return jnp.concatenate([first, rest], axis=axis_number)


def reference(grad_pressure, beta, tile_rows, tile_owner, tile_slot, face_mask, heights):
    beta_x, beta_y, beta_z = beta[0], beta[1], beta[2]
    low_x = shifted_low(beta_x, 0)
    low_y = shifted_low(beta_y, 1)
    low_z = shifted_low(beta_z, 2)
    diagonal = beta_x + low_x + beta_y + low_y + beta_z + low_z
    inv_diag = 1.0 / diagonal

    def operate(field):
        padded = jnp.pad(field, 1)
        inner = padded[1:-1, 1:-1, 1:-1]
        beside = beta_x * padded[2:, 1:-1, 1:-1] + low_x * padded[:-2, 1:-1, 1:-1]
        beside = beside + beta_y * padded[1:-1, 2:, 1:-1] + low_y * padded[1:-1, :-2, 1:-1]
        beside = beside + beta_z * padded[1:-1, 1:-1, 2:] + low_z * padded[1:-1, 1:-1, :-2]
        return diagonal * inner - beside

    adjoint = grad_pressure
    grad_rhs = jnp.zeros_like(grad_pressure)
    for cycle_index in range(ITERS):
        for step_index in reversed(range(STEPS)):
            scaled = omega_of(step_index) * inv_diag * adjoint
            grad_rhs = grad_rhs + scaled
            adjoint = adjoint - operate(scaled)

    peers = N_GX * N_GY
    blocks = NZ // 128
    device = jnp.arange(peers * NT, dtype=jnp.int32) // NT
    index_x = device // N_GY
    index_y = device % N_GY
    local_x = tile_rows // (CY * blocks)
    local_y = (tile_rows // blocks) % CY
    block_z = tile_rows % blocks
    grid_rows = grad_rhs.reshape(NX, NY, blocks, 128)
    picked = grid_rows[index_x * CX + local_x, index_y * CY + local_y, block_z]
    jump = face_mask.astype(jnp.float32) * picked
    global_slot = (tile_owner[:, 0] * SLOTS + tile_slot).astype(jnp.int32)
    table = jnp.zeros((peers * SLOTS, 128), jnp.float32).at[global_slot].add(jump)

    slope = 0.5 * (heights[2] - heights[0])
    bend = heights[2] - 2.0 * heights[1] + heights[0]
    denom = 1.0 + slope * slope
    factor = denom ** -1.5
    skew_term = -3.0 * slope * bend * denom ** -2.5
    grad_heights = jnp.stack([table * (factor - 0.5 * skew_term), -2.0 * table * factor, table * (factor + 0.5 * skew_term)])
    return grad_rhs, grad_heights
```

```python
import functools
import math

import jax
import jax.numpy as jnp
from jax import lax
from jax.experimental import pallas as pl
from jax.experimental.pallas import tpu as pltpu
from jax.sharding import PartitionSpec as P

ITERS = 3
STEPS = 4
CAP = 8
LANES = 128
ROWS = 8

LOW_BOUND = 0.1
HIGH_BOUND = 1.9

MESH = pl.DeviceIdType.MESH
EXACT = lax.Precision.HIGHEST


def omega_of(step_index):
    theta = 0.5 * (HIGH_BOUND + LOW_BOUND) + 0.5 * (HIGH_BOUND - LOW_BOUND) * math.cos(
        math.pi * (2 * step_index + 1) / (2 * STEPS)
    )
    return 1.0 / theta


def omega_at(step):
    j = STEPS - 1 - step % STEPS
    value = jnp.float32(omega_of(0))
    for index in range(1, STEPS):
        value = jnp.where(j == index, jnp.float32(omega_of(index)), value)
    return value


def kernel(
    n_x, n_y,
    grad_ref, beta_ref, rows_ref, owner_ref, slot_ref, mask_ref, heights_ref,
    out_ref, back_ref,
    coeff, state, halo_x, halo_y, face_y, rim_x, rim_y, rim_face,
    flat, picked, place, send_rows, recv_rows, send_slots, recv_slots,
    rim_send, rim_recv, x_send, x_recv, y_send, y_recv, row_send, row_recv, slot_send, slot_recv,
):
    X, Y, Z = grad_ref.shape
    groups = Y // ROWS
    blocks = Z // LANES
    tiles = rows_ref.shape[0]
    peers = n_x * n_y
    slots = heights_ref.shape[1]
    ix = lax.axis_index("gx")
    iy = lax.axis_index("gy")
    me = ix * n_y + iy
    has_x = (ix > 0, ix < n_x - 1)
    has_y = (iy > 0, iy < n_y - 1)
    at_x = ((ix - 1, iy), (ix + 1, iy))
    at_y = ((ix, iy - 1), (ix, iy + 1))

    rim_x[...] = jnp.zeros_like(rim_x)
    rim_y[...] = jnp.zeros_like(rim_y)
    halo_x[...] = jnp.zeros_like(halo_x)
    halo_y[...] = jnp.zeros_like(halo_y)

    def peer_at(step):
        peer = (me + step) % peers
        return peer, (peer // n_y, peer % n_y)

    barrier = pltpu.get_barrier_semaphore()

    @pl.loop(1, peers)
    def _(step):
        pl.semaphore_signal(barrier, inc=1, device_id=peer_at(step)[1], device_id_type=MESH)

    for x in range(X):
        rim_face[x : x + 1, :] = beta_ref[1, x, Y - 1 : Y, :]

    owner = owner_ref[...]
    peer_ids = lax.broadcasted_iota(jnp.int32, (tiles, peers), 1)
    named = (owner == peer_ids).astype(jnp.float32)
    before = lax.broadcasted_iota(jnp.int32, (tiles, tiles), 0)
    after = lax.broadcasted_iota(jnp.int32, (tiles, tiles), 1)
    earlier = (after < before).astype(jnp.float32)
    counts = jnp.dot(earlier, named, preferred_element_type=jnp.float32, precision=EXACT)
    position = jnp.sum(counts * named, axis=1, keepdims=True)
    target = owner.astype(jnp.float32) * CAP + position
    columns = lax.broadcasted_iota(jnp.int32, (tiles, peers * CAP), 1).astype(jnp.float32)
    place[...] = (target == columns).astype(jnp.float32)
    slot_row = slot_ref[...].astype(jnp.float32)
    slot_column = jnp.sum(jnp.where(before == after, slot_row, 0.0), axis=1, keepdims=True)
    lanes = lax.broadcasted_iota(jnp.int32, (tiles, LANES), 1).astype(jnp.float32)
    spread = jnp.where(position == lanes, slot_column, 0.0)
    slot_rows = lax.dot_general(
        named, spread, (((0,), (0,)), ((), ())), preferred_element_type=jnp.float32, precision=EXACT
    )
    send_slots[...] = slot_rows.reshape(peers, 1, LANES)

    pl.semaphore_wait(barrier, peers - 1)

    def rim_copies():
        return (
            (has_x, pltpu.make_async_remote_copy(
                beta_ref.at[0, X - 1], rim_x, rim_send.at[0], rim_recv.at[0],
                device_id=at_x[1], device_id_type=MESH)),
            (has_y, pltpu.make_async_remote_copy(
                rim_face, rim_y, rim_send.at[1], rim_recv.at[1],
                device_id=at_y[1], device_id_type=MESH)),
        )

    for has, copy in rim_copies():
        @pl.when(has[1])
        def _():
            copy.start()

    def slot_copy(step):
        peer, place_of = peer_at(step)
        return pltpu.make_async_remote_copy(
            send_slots.at[peer], recv_slots.at[me], slot_send.at[peer], slot_recv.at[me],
            device_id=place_of, device_id_type=MESH)

    def row_copy(step):
        peer, place_of = peer_at(step)
        return pltpu.make_async_remote_copy(
            send_rows.at[peer], recv_rows.at[me], row_send.at[peer], row_recv.at[me],
            device_id=place_of, device_id_type=MESH)

    def rows_of(g):
        return pl.ds(g * ROWS, ROWS)

    def x_copy(par, side, g):
        return pltpu.make_async_remote_copy(
            state.at[par, (X - 1) * side, rows_of(g)], halo_x.at[par, 1 - side, rows_of(g)],
            x_send.at[par, side, g], x_recv.at[par, 1 - side, g],
            device_id=at_x[side], device_id_type=MESH)

    def y_copy(par, side):
        return pltpu.make_async_remote_copy(
            face_y.at[par, side], halo_y.at[par, 1 - side],
            y_send.at[par, side], y_recv.at[par, 1 - side],
            device_id=at_y[side], device_id_type=MESH)

    def x_arrival(par, side, g):
        return pltpu.make_async_remote_copy(
            state.at[par, 0, rows_of(g)], halo_x.at[par, side, rows_of(g)],
            x_send.at[par, side, g], x_recv.at[par, side, g],
            device_id=at_x[side], device_id_type=MESH)

    def y_arrival(par, side):
        return pltpu.make_async_remote_copy(
            face_y.at[par, side], halo_y.at[par, side],
            y_send.at[par, side], y_recv.at[par, side],
            device_id=at_y[side], device_id_type=MESH)

    row_ids = lax.broadcasted_iota(jnp.int32, (ROWS, Z), 0)
    z_ids = lax.broadcasted_iota(jnp.int32, (ROWS, Z), 1)

    def from_below(tile, row):
        return jnp.where(row_ids == 0, row, pltpu.roll(tile, 1, 0))

    def from_above(tile, row):
        return jnp.where(row_ids == ROWS - 1, row, pltpu.roll(tile, ROWS - 1, 0))

    first = omega_at(0)

    def prepare(x, g):
        r = slice(g * ROWS, (g + 1) * ROWS)
        up_x, up_y, up_z = beta_ref[0, x, r, :], beta_ref[1, x, r, :], beta_ref[2, x, r, :]
        low_x = rim_x[r, :] if x == 0 else beta_ref[0, x - 1, r, :]
        row = rim_y[x : x + 1, :] if g == 0 else beta_ref[1, x, g * ROWS - 1 : g * ROWS, :]
        low_y = from_below(up_y, row)
        low_z = jnp.where(z_ids == 0, 0.0, pltpu.roll(up_z, 1, 1))
        inv = 1.0 / (up_x + low_x + up_y + low_y + up_z + low_z)
        up_z = jnp.where(z_ids == Z - 1, 0.0, up_z)
        for index, value in enumerate((up_x, low_x, up_y, low_y, up_z, low_z)):
            coeff[index, x, r, :] = value * inv
        value = inv * grad_ref[x, r, :]
        state[0, x, r, :] = value
        out_ref[x, r, :] = first * value
        if g == 0:
            face_y[0, 0, x : x + 1, :] = value[:1, :]
        if g == groups - 1:
            face_y[0, 1, x : x + 1, :] = value[ROWS - 1 :, :]

    for x in range(1, X):
        for g in range(1, groups):
            prepare(x, g)
    (_, rim_x_copy), (_, rim_y_copy) = rim_copies()

    @pl.when(has_x[0])
    def _():
        rim_x_copy.wait_recv()

    for g in range(1, groups):
        prepare(0, g)
        for side in range(2):
            @pl.when(has_x[side])
            def _():
                x_copy(0, side, g).start()

    @pl.when(has_y[0])
    def _():
        rim_y_copy.wait_recv()

    @pl.when(has_y[1])
    def _():
        y_copy(0, 1).start()

    prepare(0, 0)
    prepare(X - 1, 0)
    for side in range(2):
        @pl.when(has_x[side])
        def _():
            x_copy(0, side, 0).start()
    for x in range(1, X - 1):
        prepare(x, 0)

    @pl.when(has_y[0])
    def _():
        y_copy(0, 0).start()

    for has, copy in rim_copies():
        @pl.when(has[1])
        def _():
            copy.wait_send()

    @pl.loop(1, peers)
    def _(step):
        slot_copy(step).start()

    recv_slots[me] = send_slots[me]

    total = ITERS * STEPS

    def update(par, omega, weight, x, g):
        r = slice(g * ROWS, (g + 1) * ROWS)
        s = state[par, x, r, :]
        above_x = halo_x[par, 1, r, :] if x == X - 1 else state[par, x + 1, r, :]
        below_x = halo_x[par, 0, r, :] if x == 0 else state[par, x - 1, r, :]
        if g == groups - 1:
            above_row = halo_y[par, 1, x : x + 1, :]
        else:
            above_row = state[par, x, (g + 1) * ROWS : (g + 1) * ROWS + 1, :]
        if g == 0:
            below_row = halo_y[par, 0, x : x + 1, :]
        else:
            below_row = state[par, x, g * ROWS - 1 : g * ROWS, :]
        beside = coeff[0, x, r, :] * above_x + coeff[1, x, r, :] * below_x
        beside += coeff[2, x, r, :] * from_above(s, above_row)
        beside += coeff[3, x, r, :] * from_below(s, below_row)
        beside += coeff[4, x, r, :] * pltpu.roll(s, Z - 1, 1)
        beside += coeff[5, x, r, :] * pltpu.roll(s, 1, 1)
        value = s + omega * (beside - s)
        state[1 - par, x, r, :] = value
        out_ref[x, r, :] += weight * value
        if g == 0:
            face_y[1 - par, 0, x : x + 1, :] = value[:1, :]
        if g == groups - 1:
            face_y[1 - par, 1, x : x + 1, :] = value[ROWS - 1 :, :]

    def finish_sends(par, go):
        for side in range(2):
            for g in range(groups):
                @pl.when(jnp.logical_and(has_x[side], go))
                def _():
                    x_copy(par, side, g).wait_send()

            @pl.when(jnp.logical_and(has_y[side], go))
            def _():
                y_copy(par, side).wait_send()

    def step_body(step, carry):
        par = step % 2
        omega, weight = omega_at(step), omega_at(step + 1)
        more = step + 2 < total
        finish_sends(1 - par, step > 0)

        def ends(g):
            for side in range(2):
                @pl.when(has_x[side])
                def _():
                    x_arrival(par, side, g).wait_recv()

                update(par, omega, weight, (X - 1) * side, g)

                @pl.when(jnp.logical_and(has_x[side], more))
                def _():
                    x_copy(1 - par, side, g).start()

        for g in range(1, groups - 1):
            ends(g)
        for side, g in ((0, 0), (1, groups - 1)):
            @pl.when(has_y[side])
            def _():
                y_arrival(par, side).wait_recv()

            ends(g)
            for x in range(1, X - 1):
                update(par, omega, weight, x, g)

            @pl.when(jnp.logical_and(has_y[side], more))
            def _():
                y_copy(1 - par, side).start()

        for x in range(1, X - 1):
            for g in range(1, groups - 1):
                update(par, omega, weight, x, g)
        return carry

    lax.fori_loop(0, total - 1, step_body, 0)
    finish_sends((total - 2) % 2, True)

    for x in range(X):
        for b in range(blocks):
            start = (x * blocks + b) * Y
            flat[start : start + Y, :] = out_ref[x, :, b * LANES : (b + 1) * LANES]

    unroll = 8

    @pl.loop(0, tiles // unroll)
    def _(chunk):
        for lane in range(unroll):
            t = chunk * unroll + lane
            row = rows_ref[t]
            x = row // (Y * blocks)
            y = (row // blocks) % Y
            at = (x * blocks + row % blocks) * Y + y
            picked[pl.ds(t, 1), :] = flat[pl.ds(at, 1), :]

    jumps = picked[...] * mask_ref[...].astype(jnp.float32)
    send_rows[...] = lax.dot_general(
        place[...], jumps, (((0,), (0,)), ((), ())),
        preferred_element_type=jnp.float32, precision=EXACT,
    ).reshape(peers, CAP, LANES)

    @pl.loop(1, peers)
    def _(step):
        row_copy(step).start()

    recv_rows[me] = send_rows[me]

    @pl.loop(1, peers)
    def _(step):
        peer, place_of = peer_at(step)
        pltpu.make_async_remote_copy(
            send_slots.at[peer], recv_slots.at[peer], slot_send.at[peer], slot_recv.at[peer],
            device_id=place_of, device_id_type=MESH).wait()

    own = lax.broadcasted_iota(jnp.int32, (peers, CAP, LANES), 1)
    lane_ids = lax.broadcasted_iota(jnp.int32, (peers, CAP, LANES), 2)
    got = jnp.broadcast_to(recv_slots[...], (peers, CAP, LANES))
    slot_of = jnp.sum(jnp.where(own == lane_ids, got, 0.0), axis=2, keepdims=True)
    slot_of = slot_of.reshape(peers * CAP, 1)
    slot_ids = lax.broadcasted_iota(jnp.int32, (peers * CAP, slots), 1).astype(jnp.float32)
    chosen = (slot_of == slot_ids).astype(jnp.float32)

    slope = 0.5 * (heights_ref[2] - heights_ref[0])
    bend = heights_ref[2] - 2.0 * heights_ref[1] + heights_ref[0]
    denom = 1.0 + slope * slope
    factor = 1.0 / (denom * jnp.sqrt(denom))
    skew = -3.0 * slope * bend * factor / denom

    @pl.loop(1, peers)
    def _(step):
        peer, place_of = peer_at(step)
        pltpu.make_async_remote_copy(
            send_rows.at[peer], recv_rows.at[peer], row_send.at[peer], row_recv.at[peer],
            device_id=place_of, device_id_type=MESH).wait()

    table = lax.dot_general(
        chosen, recv_rows[...].reshape(peers * CAP, LANES), (((0,), (0,)), ((), ())),
        preferred_element_type=jnp.float32, precision=EXACT,
    )
    back_ref[0] = table * (factor - 0.5 * skew)
    back_ref[1] = -2.0 * table * factor
    back_ref[2] = table * (factor + 0.5 * skew)


def shards(grad_pressure, beta, tile_rows, tile_owner, tile_slot, face_mask, heights):
    n_x, n_y = lax.axis_size("gx"), lax.axis_size("gy")
    peers = n_x * n_y
    X, Y, Z = grad_pressure.shape
    groups = Y // ROWS
    tiles = tile_rows.shape[0]
    f32 = jnp.float32
    vmem = pl.BlockSpec(memory_space=pltpu.VMEM)
    smem = pl.BlockSpec(memory_space=pltpu.SMEM)
    dma = pltpu.SemaphoreType.DMA
    return pl.pallas_call(
        functools.partial(kernel, n_x, n_y),
        out_shape=(
            jax.ShapeDtypeStruct((X, Y, Z), f32),
            jax.ShapeDtypeStruct(heights.shape, f32),
        ),
        in_specs=[vmem, vmem, smem, vmem, vmem, vmem, vmem],
        out_specs=(vmem, vmem),
        scratch_shapes=[
            pltpu.VMEM((6, X, Y, Z), f32),
            pltpu.VMEM((2, X, Y, Z), f32),
            pltpu.VMEM((2, 2, Y, Z), f32),
            pltpu.VMEM((2, 2, X, Z), f32),
            pltpu.VMEM((2, 2, X, Z), f32),
            pltpu.VMEM((Y, Z), f32),
            pltpu.VMEM((X, Z), f32),
            pltpu.VMEM((X, Z), f32),
            pltpu.VMEM((X * Y * Z // LANES, LANES), f32),
            pltpu.VMEM((tiles, LANES), f32),
            pltpu.VMEM((tiles, peers * CAP), f32),
            pltpu.VMEM((peers, CAP, LANES), f32),
            pltpu.VMEM((peers, CAP, LANES), f32),
            pltpu.VMEM((peers, 1, LANES), f32),
            pltpu.VMEM((peers, 1, LANES), f32),
            dma((2,)),
            dma((2,)),
            dma((2, 2, groups)),
            dma((2, 2, groups)),
            dma((2, 2)),
            dma((2, 2)),
            dma((peers,)),
            dma((peers,)),
            dma((peers,)),
            dma((peers,)),
        ],
        compiler_params=pltpu.CompilerParams(
            collective_id=0, has_side_effects=True, vmem_limit_bytes=56 * 1024 * 1024
        ),
    )(grad_pressure, beta, tile_rows, tile_owner, tile_slot.reshape(1, -1), face_mask, heights)


def solution(mesh):
    in_specs = (
        P("gx", "gy", None),
        P(None, "gx", "gy", None),
        P(("gx", "gy")),
        P(("gx", "gy"), None),
        P(("gx", "gy")),
        P(("gx", "gy"), None),
        P(None, ("gx", "gy"), None),
    )
    out_specs = (P("gx", "gy", None), P(None, ("gx", "gy"), None))
    return jax.shard_map(shards, mesh=mesh, in_specs=in_specs, out_specs=out_specs, check_vma=False)
```

```python
import functools
import math

import jax
import jax.numpy as jnp
from jax import lax
from jax.experimental import pallas as pl
from jax.experimental.pallas import tpu as pltpu
from jax.sharding import PartitionSpec as P

ITERS = 3
STEPS = 4
CAP = 8
LANES = 128
ROWS = 8

LOW_BOUND = 0.1
HIGH_BOUND = 1.9

MESH = pl.DeviceIdType.MESH
EXACT = lax.Precision.HIGHEST


def omega_of(step_index):
    theta = 0.5 * (HIGH_BOUND + LOW_BOUND) + 0.5 * (HIGH_BOUND - LOW_BOUND) * math.cos(
        math.pi * (2 * step_index + 1) / (2 * STEPS)
    )
    return 1.0 / theta


def omega_at(step):
    j = STEPS - 1 - step % STEPS
    value = jnp.float32(omega_of(0))
    for index in range(1, STEPS):
        value = jnp.where(j == index, jnp.float32(omega_of(index)), value)
    return value


def picked_sum(selector, rows):
    high = rows.astype(jnp.bfloat16)
    rest = rows - high.astype(jnp.float32)
    middle = rest.astype(jnp.bfloat16)
    low = (rest - middle.astype(jnp.float32)).astype(jnp.bfloat16)
    parts = [jnp.dot(selector, part, preferred_element_type=jnp.float32) for part in (high, middle, low)]
    return parts[0] + (parts[1] + parts[2])


def kernel(
    n_x, n_y,
    grad_ref, beta_ref, rows_ref, owner_ref, slot_ref, mask_ref, heights_ref,
    out_ref, back_ref,
    coeff, state, halo_x, halo_y, face_y, rim_x, rim_y, rim_face, face_coeff,
    flat, picked, place, send_rows, recv_rows, send_slots, recv_slots,
    rim_send, rim_recv, x_send, x_recv, y_send, y_recv, row_send, row_recv, slot_send, slot_recv,
):
    X, Y, Z = grad_ref.shape
    groups = Y // ROWS
    blocks = Z // LANES
    tiles = rows_ref.shape[0]
    peers = n_x * n_y
    slots = heights_ref.shape[1]
    ix = lax.axis_index("gx")
    iy = lax.axis_index("gy")
    me = ix * n_y + iy
    has_x = (ix > 0, ix < n_x - 1)
    has_y = (iy > 0, iy < n_y - 1)
    at_x = ((ix - 1, iy), (ix + 1, iy))
    at_y = ((ix, iy - 1), (ix, iy + 1))

    rim_x[...] = jnp.zeros_like(rim_x)
    rim_y[...] = jnp.zeros_like(rim_y)
    halo_x[...] = jnp.zeros_like(halo_x)
    halo_y[...] = jnp.zeros_like(halo_y)

    def peer_at(step):
        peer = (me + step) % peers
        return peer, (peer // n_y, peer % n_y)

    barrier = pltpu.get_barrier_semaphore()

    @pl.loop(1, peers)
    def _(step):
        pl.semaphore_signal(barrier, inc=1, device_id=peer_at(step)[1], device_id_type=MESH)

    for x in range(X):
        rim_face[x : x + 1, :] = beta_ref[1, x, Y - 1 : Y, :]

    owner = owner_ref[...]
    peer_ids = lax.broadcasted_iota(jnp.int32, (peers, tiles), 0)
    named = (owner == peer_ids).astype(jnp.float32)
    down = lax.broadcasted_iota(jnp.int32, (tiles, tiles), 0)
    across = lax.broadcasted_iota(jnp.int32, (tiles, tiles), 1)
    earlier = (down < across).astype(jnp.bfloat16)
    counts = jnp.dot(named.astype(jnp.bfloat16), earlier, preferred_element_type=jnp.float32)
    position = jnp.sum(counts * named, axis=0, keepdims=True)
    target = owner.astype(jnp.float32) * CAP + position
    spots = lax.broadcasted_iota(jnp.int32, (peers * CAP, tiles), 0).astype(jnp.float32)
    place[...] = (target == spots).astype(jnp.float32).astype(jnp.bfloat16)
    spread = lax.broadcasted_iota(jnp.int32, (LANES, tiles), 0).astype(jnp.float32)
    spread = (spread == position).astype(jnp.float32)
    slot_rows = lax.dot_general(
        named * slot_ref[...].astype(jnp.float32), spread, (((1,), (1,)), ((), ())),
        preferred_element_type=jnp.float32, precision=EXACT,
    )
    send_slots[...] = slot_rows.reshape(peers, 1, LANES)

    pl.semaphore_wait(barrier, peers - 1)

    def rim_copies():
        return (
            (has_x, pltpu.make_async_remote_copy(
                beta_ref.at[0, X - 1], rim_x, rim_send.at[0], rim_recv.at[0],
                device_id=at_x[1], device_id_type=MESH)),
            (has_y, pltpu.make_async_remote_copy(
                rim_face, rim_y, rim_send.at[1], rim_recv.at[1],
                device_id=at_y[1], device_id_type=MESH)),
        )

    for has, copy in rim_copies():
        @pl.when(has[1])
        def _():
            copy.start()

    def slot_copy(step):
        peer, place_of = peer_at(step)
        return pltpu.make_async_remote_copy(
            send_slots.at[peer], recv_slots.at[me], slot_send.at[peer], slot_recv.at[me],
            device_id=place_of, device_id_type=MESH)

    def row_copy(step):
        peer, place_of = peer_at(step)
        return pltpu.make_async_remote_copy(
            send_rows.at[peer], recv_rows.at[me], row_send.at[peer], row_recv.at[me],
            device_id=place_of, device_id_type=MESH)

    def rows_of(g):
        return pl.ds(g * ROWS, ROWS)

    def x_copy(par, side, g):
        return pltpu.make_async_remote_copy(
            state.at[par, (X - 1) * side, rows_of(g)], halo_x.at[par, 1 - side, rows_of(g)],
            x_send.at[par, side, g], x_recv.at[par, 1 - side, g],
            device_id=at_x[side], device_id_type=MESH)

    def y_copy(par, side):
        return pltpu.make_async_remote_copy(
            face_y.at[par, side], halo_y.at[par, 1 - side],
            y_send.at[par, side], y_recv.at[par, 1 - side],
            device_id=at_y[side], device_id_type=MESH)

    def x_arrival(par, side, g):
        return pltpu.make_async_remote_copy(
            state.at[par, 0, rows_of(g)], halo_x.at[par, side, rows_of(g)],
            x_send.at[par, side, g], x_recv.at[par, side, g],
            device_id=at_x[side], device_id_type=MESH)

    def y_arrival(par, side):
        return pltpu.make_async_remote_copy(
            face_y.at[par, side], halo_y.at[par, side],
            y_send.at[par, side], y_recv.at[par, side],
            device_id=at_y[side], device_id_type=MESH)

    row_ids = lax.broadcasted_iota(jnp.int32, (ROWS, Z), 0)
    z_ids = lax.broadcasted_iota(jnp.int32, (ROWS, Z), 1)

    def from_below(tile, row):
        return jnp.where(row_ids == 0, row, pltpu.roll(tile, 1, 0))

    def from_above(tile, row):
        return jnp.where(row_ids == ROWS - 1, row, pltpu.roll(tile, ROWS - 1, 0))

    def prepare(x, g):
        r = slice(g * ROWS, (g + 1) * ROWS)
        up_x, up_y, up_z = beta_ref[0, x, r, :], beta_ref[1, x, r, :], beta_ref[2, x, r, :]
        low_x = rim_x[r, :] if x == 0 else beta_ref[0, x - 1, r, :]
        row = rim_y[x : x + 1, :] if g == 0 else beta_ref[1, x, g * ROWS - 1 : g * ROWS, :]
        low_y = from_below(up_y, row)
        low_z = jnp.where(z_ids == 0, 0.0, pltpu.roll(up_z, 1, 1))
        inv = 1.0 / (up_x + low_x + up_y + low_y + up_z + low_z)
        up_z = jnp.where(z_ids == Z - 1, 0.0, up_z)
        for index, value in enumerate((up_x, low_x, up_y, low_y, up_z, low_z)):
            value = value * inv
            coeff[index, x, r, :] = value
            if index == 3 and g == 0:
                face_coeff[0, x : x + 1, :] = value[:1, :]
            if index == 2 and g == groups - 1:
                face_coeff[1, x : x + 1, :] = value[ROWS - 1 :, :]
        value = inv * grad_ref[x, r, :]
        state[0, x, r, :] = value
        out_ref[x, r, :] = jnp.zeros_like(value)
        if g == 0:
            face_y[0, 0, x : x + 1, :] = value[:1, :]
        if g == groups - 1:
            face_y[0, 1, x : x + 1, :] = value[ROWS - 1 :, :]

    for x in range(1, X):
        for g in range(1, groups):
            prepare(x, g)
    (_, rim_x_copy), (_, rim_y_copy) = rim_copies()

    @pl.when(has_x[0])
    def _():
        rim_x_copy.wait_recv()

    for g in range(1, groups):
        prepare(0, g)
        for side in range(2):
            @pl.when(has_x[side])
            def _():
                x_copy(0, side, g).start()

    @pl.when(has_y[0])
    def _():
        rim_y_copy.wait_recv()

    @pl.when(has_y[1])
    def _():
        y_copy(0, 1).start()

    prepare(0, 0)
    prepare(X - 1, 0)
    for side in range(2):
        @pl.when(has_x[side])
        def _():
            x_copy(0, side, 0).start()
    for x in range(1, X - 1):
        prepare(x, 0)

    @pl.when(has_y[0])
    def _():
        y_copy(0, 0).start()

    for has, copy in rim_copies():
        @pl.when(has[1])
        def _():
            copy.wait_send()

    @pl.loop(1, peers)
    def _(step):
        slot_copy(step).start()

    recv_slots[me] = send_slots[me]

    total = ITERS * STEPS

    def faces_of(par, value, x, g):
        if g == 0:
            face_y[par, 0, x : x + 1, :] = value[:1, :]
        if g == groups - 1:
            face_y[par, 1, x : x + 1, :] = value[ROWS - 1 :, :]

    def update(par, omega, x, g):
        r = slice(g * ROWS, (g + 1) * ROWS)
        s = state[par, x, r, :]
        out_ref[x, r, :] += omega * s
        if g == groups - 1:
            above_row = 0.0
        else:
            above_row = state[par, x, (g + 1) * ROWS : (g + 1) * ROWS + 1, :]
        if g == 0:
            below_row = 0.0
        else:
            below_row = state[par, x, g * ROWS - 1 : g * ROWS, :]
        beside = coeff[2, x, r, :] * from_above(s, above_row)
        beside += coeff[3, x, r, :] * from_below(s, below_row)
        beside += coeff[4, x, r, :] * pltpu.roll(s, Z - 1, 1)
        beside += coeff[5, x, r, :] * pltpu.roll(s, 1, 1)
        if x < X - 1:
            beside += coeff[0, x, r, :] * state[par, x + 1, r, :]
        if x > 0:
            beside += coeff[1, x, r, :] * state[par, x - 1, r, :]
        value = s + omega * (beside - s)
        state[1 - par, x, r, :] = value
        if 0 < x < X - 1:
            faces_of(1 - par, value, x, g)

    def add_halo_x(par, omega, side, g):
        @pl.when(has_x[side])
        def _():
            x_arrival(par, side, g).wait_recv()

        x = (X - 1) * side
        r = slice(g * ROWS, (g + 1) * ROWS)
        value = state[1 - par, x, r, :] + omega * (coeff[1 - side, x, r, :] * halo_x[par, side, r, :])
        state[1 - par, x, r, :] = value
        faces_of(1 - par, value, x, g)

    def finish_sends(par, go):
        for side in range(2):
            for g in range(groups):
                @pl.when(jnp.logical_and(has_x[side], go))
                def _():
                    x_copy(par, side, g).wait_send()

            @pl.when(jnp.logical_and(has_y[side], go))
            def _():
                y_copy(par, side).wait_send()

    def step_body(step, carry):
        par = step % 2
        omega = omega_at(step)
        more = step + 2 < total
        finish_sends(1 - par, step > 0)
        for x in range(X):
            for g in range(groups):
                update(par, omega, x, g)

        def send_x(side, g):
            @pl.when(jnp.logical_and(has_x[side], more))
            def _():
                x_copy(1 - par, side, g).start()

        for g in range(1, groups - 1):
            for side in range(2):
                add_halo_x(par, omega, side, g)
                send_x(side, g)
        ends = (0, groups - 1)
        for g in ends:
            for side in range(2):
                add_halo_x(par, omega, side, g)
        for side in range(2):
            @pl.when(has_y[side])
            def _():
                y_arrival(par, side).wait_recv()

            face = face_y[1 - par, side] + omega * (face_coeff[side] * halo_y[par, side])
            face_y[1 - par, side] = face

            @pl.when(jnp.logical_and(has_y[side], more))
            def _():
                y_copy(1 - par, side).start()

            row = (Y - 1) * side
            for x in range(X):
                state[1 - par, x, row : row + 1, :] = face[x : x + 1, :]
            for x_side in range(2):
                send_x(x_side, ends[side])
        return carry

    lax.fori_loop(0, total - 1, step_body, 0)
    finish_sends((total - 2) % 2, True)

    last = omega_of(STEPS - 1 - (total - 1) % STEPS)

    for x in range(X):
        for b in range(blocks):
            start = (x * blocks + b) * Y
            cut = slice(b * LANES, (b + 1) * LANES)
            value = out_ref[x, :, cut] + last * state[(total - 1) % 2, x, :, cut]
            out_ref[x, :, cut] = value
            flat[start : start + Y, :] = value

    unroll = 8

    @pl.loop(0, tiles // unroll)
    def _(chunk):
        for lane in range(unroll):
            t = chunk * unroll + lane
            row = rows_ref[t]
            line = lax.div(row, blocks)
            x = lax.div(line, Y)
            at = (x * blocks + row - line * blocks) * Y + line - x * Y
            picked[pl.ds(t, 1), :] = flat[pl.ds(at, 1), :]

    jumps = picked[...] * mask_ref[...].astype(jnp.float32)
    send_rows[...] = picked_sum(place[...], jumps).reshape(peers, CAP, LANES)

    @pl.loop(1, peers)
    def _(step):
        row_copy(step).start()

    recv_rows[me] = send_rows[me]

    @pl.loop(1, peers)
    def _(step):
        peer, place_of = peer_at(step)
        pltpu.make_async_remote_copy(
            send_slots.at[peer], recv_slots.at[peer], slot_send.at[peer], slot_recv.at[peer],
            device_id=place_of, device_id_type=MESH).wait()

    own = lax.broadcasted_iota(jnp.int32, (peers, CAP, LANES), 1)
    lane_ids = lax.broadcasted_iota(jnp.int32, (peers, CAP, LANES), 2)
    got = jnp.broadcast_to(recv_slots[...], (peers, CAP, LANES))
    slot_of = jnp.sum(jnp.where(own == lane_ids, got, 0.0), axis=2, keepdims=True)
    slot_of = slot_of.reshape(peers * CAP, 1)
    slot_ids = lax.broadcasted_iota(jnp.int32, (peers * CAP, slots), 1).astype(jnp.float32)
    chosen = (slot_of == slot_ids).astype(jnp.float32).T.astype(jnp.bfloat16)

    slope = 0.5 * (heights_ref[2] - heights_ref[0])
    bend = heights_ref[2] - 2.0 * heights_ref[1] + heights_ref[0]
    denom = 1.0 + slope * slope
    factor = 1.0 / (denom * jnp.sqrt(denom))
    skew = -3.0 * slope * bend * factor / denom

    @pl.loop(1, peers)
    def _(step):
        peer, place_of = peer_at(step)
        pltpu.make_async_remote_copy(
            send_rows.at[peer], recv_rows.at[peer], row_send.at[peer], row_recv.at[peer],
            device_id=place_of, device_id_type=MESH).wait()

    table = picked_sum(chosen, recv_rows[...].reshape(peers * CAP, LANES))
    back_ref[0] = table * (factor - 0.5 * skew)
    back_ref[1] = -2.0 * table * factor
    back_ref[2] = table * (factor + 0.5 * skew)


def shards(grad_pressure, beta, tile_rows, tile_owner, tile_slot, face_mask, heights):
    n_x, n_y = lax.axis_size("gx"), lax.axis_size("gy")
    peers = n_x * n_y
    X, Y, Z = grad_pressure.shape
    groups = Y // ROWS
    tiles = tile_rows.shape[0]
    f32 = jnp.float32
    vmem = pl.BlockSpec(memory_space=pltpu.VMEM)
    smem = pl.BlockSpec(memory_space=pltpu.SMEM)
    dma = pltpu.SemaphoreType.DMA
    return pl.pallas_call(
        functools.partial(kernel, n_x, n_y),
        out_shape=(
            jax.ShapeDtypeStruct((X, Y, Z), f32),
            jax.ShapeDtypeStruct(heights.shape, f32),
        ),
        in_specs=[vmem, vmem, smem, vmem, vmem, vmem, vmem],
        out_specs=(vmem, vmem),
        scratch_shapes=[
            pltpu.VMEM((6, X, Y, Z), f32),
            pltpu.VMEM((2, X, Y, Z), f32),
            pltpu.VMEM((2, 2, Y, Z), f32),
            pltpu.VMEM((2, 2, X, Z), f32),
            pltpu.VMEM((2, 2, X, Z), f32),
            pltpu.VMEM((Y, Z), f32),
            pltpu.VMEM((X, Z), f32),
            pltpu.VMEM((X, Z), f32),
            pltpu.VMEM((2, X, Z), f32),
            pltpu.VMEM((X * Y * Z // LANES, LANES), f32),
            pltpu.VMEM((tiles, LANES), f32),
            pltpu.VMEM((peers * CAP, tiles), jnp.bfloat16),
            pltpu.VMEM((peers, CAP, LANES), f32),
            pltpu.VMEM((peers, CAP, LANES), f32),
            pltpu.VMEM((peers, 1, LANES), f32),
            pltpu.VMEM((peers, 1, LANES), f32),
            dma((2,)),
            dma((2,)),
            dma((2, 2, groups)),
            dma((2, 2, groups)),
            dma((2, 2)),
            dma((2, 2)),
            dma((peers,)),
            dma((peers,)),
            dma((peers,)),
            dma((peers,)),
        ],
        compiler_params=pltpu.CompilerParams(
            collective_id=0, has_side_effects=True, vmem_limit_bytes=32 * 1024 * 1024
        ),
    )(grad_pressure, beta, tile_rows, tile_owner.reshape(1, -1), tile_slot.reshape(1, -1), face_mask, heights)


def solution(mesh):
    in_specs = (
        P("gx", "gy", None),
        P(None, "gx", "gy", None),
        P(("gx", "gy")),
        P(("gx", "gy"), None),
        P(("gx", "gy")),
        P(("gx", "gy"), None),
        P(None, ("gx", "gy"), None),
    )
    out_specs = (P("gx", "gy", None), P(None, ("gx", "gy"), None))
    return jax.shard_map(shards, mesh=mesh, in_specs=in_specs, out_specs=out_specs, check_vma=False)
```

```python
import functools
import math

import jax
import jax.numpy as jnp
from jax import lax
from jax.experimental import pallas as pl
from jax.experimental.pallas import tpu as pltpu
from jax.sharding import PartitionSpec as P

ITERS = 3
STEPS = 4
CAP = 8
LANES = 128
ROWS = 8

LOW_BOUND = 0.1
HIGH_BOUND = 1.9

MESH = pl.DeviceIdType.MESH
EXACT = lax.Precision.HIGHEST


def omega_of(step_index):
    theta = 0.5 * (HIGH_BOUND + LOW_BOUND) + 0.5 * (HIGH_BOUND - LOW_BOUND) * math.cos(
        math.pi * (2 * step_index + 1) / (2 * STEPS)
    )
    return 1.0 / theta


def omega_at(step):
    j = STEPS - 1 - step % STEPS
    value = jnp.float32(omega_of(0))
    for index in range(1, STEPS):
        value = jnp.where(j == index, jnp.float32(omega_of(index)), value)
    return value


def picked_sum(selector, rows):
    high = rows.astype(jnp.bfloat16)
    rest = rows - high.astype(jnp.float32)
    middle = rest.astype(jnp.bfloat16)
    low = (rest - middle.astype(jnp.float32)).astype(jnp.bfloat16)
    parts = [jnp.dot(selector, part, preferred_element_type=jnp.float32) for part in (high, middle, low)]
    return parts[0] + (parts[1] + parts[2])


def kernel(
    n_x, n_y,
    grad_in, beta_in, rows_in, owner_in, slot_in, mask_in, heights_in,
    out_hbm, back_ref,
    out_ref,
    grad_ref, beta_ref, rows_ref, owner_ref, slot_ref, mask_ref, heights_ref, load_sem,
    coeff, state, halo_x, halo_y, face_y, rim_x, rim_y, rim_face, face_coeff,
    flat, picked, place, send_rows, recv_rows, send_slots, recv_slots,
    rim_send, rim_recv, x_send, x_recv, y_send, y_recv, row_send, row_recv, slot_send, slot_recv,
):
    X, Y, Z = grad_ref.shape
    groups = Y // ROWS
    blocks = Z // LANES
    tiles = rows_ref.shape[0]
    peers = n_x * n_y
    slots = heights_ref.shape[1]
    ix = lax.axis_index("gx")
    iy = lax.axis_index("gy")
    me = ix * n_y + iy
    has_x = (ix > 0, ix < n_x - 1)
    has_y = (iy > 0, iy < n_y - 1)
    at_x = ((ix - 1, iy), (ix + 1, iy))
    at_y = ((ix, iy - 1), (ix, iy + 1))

    rim_x[...] = jnp.zeros_like(rim_x)
    rim_y[...] = jnp.zeros_like(rim_y)
    halo_x[...] = jnp.zeros_like(halo_x)
    halo_y[...] = jnp.zeros_like(halo_y)

    def peer_at(step):
        peer = (me + step) % peers
        return peer, (peer // n_y, peer % n_y)

    barrier = pltpu.get_barrier_semaphore()

    @pl.loop(1, peers)
    def _(step):
        pl.semaphore_signal(barrier, inc=1, device_id=peer_at(step)[1], device_id_type=MESH)

    names = ("owner", "slot", "beta", "grad", "rows", "mask", "heights")
    pairs = (
        (owner_in, owner_ref), (slot_in, slot_ref), (beta_in, beta_ref), (grad_in, grad_ref),
        (rows_in, rows_ref), (mask_in, mask_ref), (heights_in, heights_ref),
    )
    loads = {
        name: pltpu.make_async_copy(source, held, load_sem.at[index])
        for index, (name, (source, held)) in enumerate(zip(names, pairs))
    }
    for name in names:
        loads[name].start()
    for name in ("owner", "slot"):
        loads[name].wait()

    owner = owner_ref[...]
    peer_ids = lax.broadcasted_iota(jnp.int32, (peers, tiles), 0)
    named = (owner == peer_ids).astype(jnp.float32)
    down = lax.broadcasted_iota(jnp.int32, (tiles, tiles), 0)
    across = lax.broadcasted_iota(jnp.int32, (tiles, tiles), 1)
    earlier = (down < across).astype(jnp.bfloat16)
    counts = jnp.dot(named.astype(jnp.bfloat16), earlier, preferred_element_type=jnp.float32)
    position = jnp.sum(counts * named, axis=0, keepdims=True)
    target = owner.astype(jnp.float32) * CAP + position
    spots = lax.broadcasted_iota(jnp.int32, (peers * CAP, tiles), 0).astype(jnp.float32)
    place[...] = (target == spots).astype(jnp.float32).astype(jnp.bfloat16)
    spread = lax.broadcasted_iota(jnp.int32, (LANES, tiles), 0).astype(jnp.float32)
    spread = (spread == position).astype(jnp.float32)
    slot_rows = lax.dot_general(
        named * slot_ref[...].astype(jnp.float32), spread, (((1,), (1,)), ((), ())),
        preferred_element_type=jnp.float32, precision=EXACT,
    )
    send_slots[...] = slot_rows.reshape(peers, 1, LANES)

    loads["beta"].wait()
    for x in range(X):
        rim_face[x : x + 1, :] = beta_ref[1, x, Y - 1 : Y, :]

    pl.semaphore_wait(barrier, peers - 1)

    def rim_copies():
        return (
            (has_x, pltpu.make_async_remote_copy(
                beta_ref.at[0, X - 1], rim_x, rim_send.at[0], rim_recv.at[0],
                device_id=at_x[1], device_id_type=MESH)),
            (has_y, pltpu.make_async_remote_copy(
                rim_face, rim_y, rim_send.at[1], rim_recv.at[1],
                device_id=at_y[1], device_id_type=MESH)),
        )

    for has, copy in rim_copies():
        @pl.when(has[1])
        def _():
            copy.start()

    def slot_copy(step):
        peer, place_of = peer_at(step)
        return pltpu.make_async_remote_copy(
            send_slots.at[peer], recv_slots.at[me], slot_send.at[peer], slot_recv.at[me],
            device_id=place_of, device_id_type=MESH)

    def row_copy(step):
        peer, place_of = peer_at(step)
        return pltpu.make_async_remote_copy(
            send_rows.at[peer], recv_rows.at[me], row_send.at[peer], row_recv.at[me],
            device_id=place_of, device_id_type=MESH)

    def rows_of(g):
        return pl.ds(g * ROWS, ROWS)

    def x_copy(par, side, g):
        return pltpu.make_async_remote_copy(
            state.at[par, (X - 1) * side, rows_of(g)], halo_x.at[par, 1 - side, rows_of(g)],
            x_send.at[par, side, g], x_recv.at[par, 1 - side, g],
            device_id=at_x[side], device_id_type=MESH)

    def y_copy(par, side):
        return pltpu.make_async_remote_copy(
            face_y.at[par, side], halo_y.at[par, 1 - side],
            y_send.at[par, side], y_recv.at[par, 1 - side],
            device_id=at_y[side], device_id_type=MESH)

    def x_arrival(par, side, g):
        return pltpu.make_async_remote_copy(
            state.at[par, 0, rows_of(g)], halo_x.at[par, side, rows_of(g)],
            x_send.at[par, side, g], x_recv.at[par, side, g],
            device_id=at_x[side], device_id_type=MESH)

    def y_arrival(par, side):
        return pltpu.make_async_remote_copy(
            face_y.at[par, side], halo_y.at[par, side],
            y_send.at[par, side], y_recv.at[par, side],
            device_id=at_y[side], device_id_type=MESH)

    row_ids = lax.broadcasted_iota(jnp.int32, (ROWS, Z), 0)
    z_ids = lax.broadcasted_iota(jnp.int32, (ROWS, Z), 1)

    def from_below(tile, row):
        return jnp.where(row_ids == 0, row, pltpu.roll(tile, 1, 0))

    def from_above(tile, row):
        return jnp.where(row_ids == ROWS - 1, row, pltpu.roll(tile, ROWS - 1, 0))

    def prepare(x, g):
        r = slice(g * ROWS, (g + 1) * ROWS)
        up_x, up_y, up_z = beta_ref[0, x, r, :], beta_ref[1, x, r, :], beta_ref[2, x, r, :]
        low_x = rim_x[r, :] if x == 0 else beta_ref[0, x - 1, r, :]
        row = rim_y[x : x + 1, :] if g == 0 else beta_ref[1, x, g * ROWS - 1 : g * ROWS, :]
        low_y = from_below(up_y, row)
        low_z = jnp.where(z_ids == 0, 0.0, pltpu.roll(up_z, 1, 1))
        inv = 1.0 / (up_x + low_x + up_y + low_y + up_z + low_z)
        up_z = jnp.where(z_ids == Z - 1, 0.0, up_z)
        for index, value in enumerate((up_x, low_x, up_y, low_y, up_z, low_z)):
            value = value * inv
            coeff[index, x, r, :] = value
            if index == 3 and g == 0:
                face_coeff[0, x : x + 1, :] = value[:1, :]
            if index == 2 and g == groups - 1:
                face_coeff[1, x : x + 1, :] = value[ROWS - 1 :, :]
        value = inv * grad_ref[x, r, :]
        state[0, x, r, :] = value
        out_ref[x, r, :] = jnp.zeros_like(value)
        if g == 0:
            face_y[0, 0, x : x + 1, :] = value[:1, :]
        if g == groups - 1:
            face_y[0, 1, x : x + 1, :] = value[ROWS - 1 :, :]

    loads["grad"].wait()
    for x in range(1, X):
        for g in range(1, groups):
            prepare(x, g)
    (_, rim_x_copy), (_, rim_y_copy) = rim_copies()

    @pl.when(has_x[0])
    def _():
        rim_x_copy.wait_recv()

    for g in range(1, groups):
        prepare(0, g)
        for side in range(2):
            @pl.when(has_x[side])
            def _():
                x_copy(0, side, g).start()

    @pl.when(has_y[0])
    def _():
        rim_y_copy.wait_recv()

    @pl.when(has_y[1])
    def _():
        y_copy(0, 1).start()

    prepare(0, 0)
    prepare(X - 1, 0)
    for side in range(2):
        @pl.when(has_x[side])
        def _():
            x_copy(0, side, 0).start()
    for x in range(1, X - 1):
        prepare(x, 0)

    @pl.when(has_y[0])
    def _():
        y_copy(0, 0).start()

    for has, copy in rim_copies():
        @pl.when(has[1])
        def _():
            copy.wait_send()

    @pl.loop(1, peers)
    def _(step):
        slot_copy(step).start()

    recv_slots[me] = send_slots[me]

    total = ITERS * STEPS

    def faces_of(par, value, x, g):
        if g == 0:
            face_y[par, 0, x : x + 1, :] = value[:1, :]
        if g == groups - 1:
            face_y[par, 1, x : x + 1, :] = value[ROWS - 1 :, :]

    def update(par, omega, x, g):
        r = slice(g * ROWS, (g + 1) * ROWS)
        s = state[par, x, r, :]
        out_ref[x, r, :] += omega * s
        if g == groups - 1:
            above_row = 0.0
        else:
            above_row = state[par, x, (g + 1) * ROWS : (g + 1) * ROWS + 1, :]
        if g == 0:
            below_row = 0.0
        else:
            below_row = state[par, x, g * ROWS - 1 : g * ROWS, :]
        beside = coeff[2, x, r, :] * from_above(s, above_row)
        beside += coeff[3, x, r, :] * from_below(s, below_row)
        beside += coeff[4, x, r, :] * pltpu.roll(s, Z - 1, 1)
        beside += coeff[5, x, r, :] * pltpu.roll(s, 1, 1)
        if x < X - 1:
            beside += coeff[0, x, r, :] * state[par, x + 1, r, :]
        if x > 0:
            beside += coeff[1, x, r, :] * state[par, x - 1, r, :]
        value = s + omega * (beside - s)
        state[1 - par, x, r, :] = value
        if 0 < x < X - 1:
            faces_of(1 - par, value, x, g)

    def add_halo_x(par, omega, side, g):
        @pl.when(has_x[side])
        def _():
            x_arrival(par, side, g).wait_recv()

        x = (X - 1) * side
        r = slice(g * ROWS, (g + 1) * ROWS)
        value = state[1 - par, x, r, :] + omega * (coeff[1 - side, x, r, :] * halo_x[par, side, r, :])
        state[1 - par, x, r, :] = value
        faces_of(1 - par, value, x, g)

    def finish_sends(par, go):
        for side in range(2):
            for g in range(groups):
                @pl.when(jnp.logical_and(has_x[side], go))
                def _():
                    x_copy(par, side, g).wait_send()

            @pl.when(jnp.logical_and(has_y[side], go))
            def _():
                y_copy(par, side).wait_send()

    def step_body(step, carry):
        par = step % 2
        omega = omega_at(step)
        more = step + 2 < total
        finish_sends(1 - par, step > 0)
        for x in range(X):
            for g in range(groups):
                update(par, omega, x, g)

        def send_x(side, g):
            @pl.when(jnp.logical_and(has_x[side], more))
            def _():
                x_copy(1 - par, side, g).start()

        for g in range(1, groups - 1):
            for side in range(2):
                add_halo_x(par, omega, side, g)
                send_x(side, g)
        ends = (0, groups - 1)
        for g in ends:
            for side in range(2):
                add_halo_x(par, omega, side, g)
        for side in range(2):
            @pl.when(has_y[side])
            def _():
                y_arrival(par, side).wait_recv()

            face = face_y[1 - par, side] + omega * (face_coeff[side] * halo_y[par, side])
            face_y[1 - par, side] = face

            @pl.when(jnp.logical_and(has_y[side], more))
            def _():
                y_copy(1 - par, side).start()

            row = (Y - 1) * side
            for x in range(X):
                state[1 - par, x, row : row + 1, :] = face[x : x + 1, :]
            for x_side in range(2):
                send_x(x_side, ends[side])
        return carry

    lax.fori_loop(0, total - 1, step_body, 0)
    finish_sends((total - 2) % 2, True)
    for name in ("rows", "mask", "heights"):
        loads[name].wait()

    last = omega_of(STEPS - 1 - (total - 1) % STEPS)

    for x in range(X):
        for b in range(blocks):
            start = (x * blocks + b) * Y
            cut = slice(b * LANES, (b + 1) * LANES)
            value = out_ref[x, :, cut] + last * state[(total - 1) % 2, x, :, cut]
            out_ref[x, :, cut] = value
            flat[start : start + Y, :] = value

    store = pltpu.make_async_copy(out_ref, out_hbm, load_sem.at[7])
    store.start()
    unroll = 8

    @pl.loop(0, tiles // unroll)
    def _(chunk):
        for lane in range(unroll):
            t = chunk * unroll + lane
            row = rows_ref[t]
            line = lax.div(row, blocks)
            x = lax.div(line, Y)
            at = (x * blocks + row - line * blocks) * Y + line - x * Y
            picked[pl.ds(t, 1), :] = flat[pl.ds(at, 1), :]

    jumps = picked[...] * mask_ref[...].astype(jnp.float32)
    send_rows[...] = picked_sum(place[...], jumps).reshape(peers, CAP, LANES)

    @pl.loop(1, peers)
    def _(step):
        row_copy(step).start()

    recv_rows[me] = send_rows[me]

    @pl.loop(1, peers)
    def _(step):
        peer, place_of = peer_at(step)
        pltpu.make_async_remote_copy(
            send_slots.at[peer], recv_slots.at[peer], slot_send.at[peer], slot_recv.at[peer],
            device_id=place_of, device_id_type=MESH).wait()

    own = lax.broadcasted_iota(jnp.int32, (peers, CAP, LANES), 1)
    lane_ids = lax.broadcasted_iota(jnp.int32, (peers, CAP, LANES), 2)
    got = jnp.broadcast_to(recv_slots[...], (peers, CAP, LANES))
    slot_of = jnp.sum(jnp.where(own == lane_ids, got, 0.0), axis=2, keepdims=True)
    slot_of = slot_of.reshape(peers * CAP, 1)
    slot_ids = lax.broadcasted_iota(jnp.int32, (peers * CAP, slots), 1).astype(jnp.float32)
    chosen = (slot_of == slot_ids).astype(jnp.float32).T.astype(jnp.bfloat16)

    slope = 0.5 * (heights_ref[2] - heights_ref[0])
    bend = heights_ref[2] - 2.0 * heights_ref[1] + heights_ref[0]
    denom = 1.0 + slope * slope
    factor = 1.0 / (denom * jnp.sqrt(denom))
    skew = -3.0 * slope * bend * factor / denom

    @pl.loop(1, peers)
    def _(step):
        peer, place_of = peer_at(step)
        pltpu.make_async_remote_copy(
            send_rows.at[peer], recv_rows.at[peer], row_send.at[peer], row_recv.at[peer],
            device_id=place_of, device_id_type=MESH).wait()

    table = picked_sum(chosen, recv_rows[...].reshape(peers * CAP, LANES))
    back_ref[0] = table * (factor - 0.5 * skew)
    back_ref[1] = -2.0 * table * factor
    back_ref[2] = table * (factor + 0.5 * skew)
    store.wait()


def shards(grad_pressure, beta, tile_rows, tile_owner, tile_slot, face_mask, heights):
    n_x, n_y = lax.axis_size("gx"), lax.axis_size("gy")
    peers = n_x * n_y
    X, Y, Z = grad_pressure.shape
    groups = Y // ROWS
    tiles = tile_rows.shape[0]
    f32 = jnp.float32
    vmem = pl.BlockSpec(memory_space=pltpu.VMEM)
    hbm = pl.BlockSpec(memory_space=pltpu.HBM)
    dma = pltpu.SemaphoreType.DMA
    return pl.pallas_call(
        functools.partial(kernel, n_x, n_y),
        out_shape=(
            jax.ShapeDtypeStruct((X, Y, Z), f32),
            jax.ShapeDtypeStruct(heights.shape, f32),
        ),
        in_specs=[hbm] * 7,
        out_specs=(hbm, vmem),
        scratch_shapes=[
            pltpu.VMEM((X, Y, Z), f32),
            pltpu.VMEM((X, Y, Z), f32),
            pltpu.VMEM(beta.shape, f32),
            pltpu.SMEM((tiles,), jnp.int32),
            pltpu.VMEM((1, tiles), jnp.int32),
            pltpu.VMEM((1, tiles), jnp.int32),
            pltpu.VMEM(face_mask.shape, jnp.int32),
            pltpu.VMEM(heights.shape, f32),
            dma((8,)),
            pltpu.VMEM((6, X, Y, Z), f32),
            pltpu.VMEM((2, X, Y, Z), f32),
            pltpu.VMEM((2, 2, Y, Z), f32),
            pltpu.VMEM((2, 2, X, Z), f32),
            pltpu.VMEM((2, 2, X, Z), f32),
            pltpu.VMEM((Y, Z), f32),
            pltpu.VMEM((X, Z), f32),
            pltpu.VMEM((X, Z), f32),
            pltpu.VMEM((2, X, Z), f32),
            pltpu.VMEM((X * Y * Z // LANES, LANES), f32),
            pltpu.VMEM((tiles, LANES), f32),
            pltpu.VMEM((peers * CAP, tiles), jnp.bfloat16),
            pltpu.VMEM((peers, CAP, LANES), f32),
            pltpu.VMEM((peers, CAP, LANES), f32),
            pltpu.VMEM((peers, 1, LANES), f32),
            pltpu.VMEM((peers, 1, LANES), f32),
            dma((2,)),
            dma((2,)),
            dma((2, 2, groups)),
            dma((2, 2, groups)),
            dma((2, 2)),
            dma((2, 2)),
            dma((peers,)),
            dma((peers,)),
            dma((peers,)),
            dma((peers,)),
        ],
        compiler_params=pltpu.CompilerParams(
            collective_id=0, has_side_effects=True, vmem_limit_bytes=56 * 1024 * 1024
        ),
    )(grad_pressure, beta, tile_rows, tile_owner.reshape(1, -1), tile_slot.reshape(1, -1), face_mask, heights)


def solution(mesh):
    in_specs = (
        P("gx", "gy", None),
        P(None, "gx", "gy", None),
        P(("gx", "gy")),
        P(("gx", "gy"), None),
        P(("gx", "gy")),
        P(("gx", "gy"), None),
        P(None, ("gx", "gy"), None),
    )
    out_specs = (P("gx", "gy", None), P(None, ("gx", "gy"), None))
    return jax.shard_map(shards, mesh=mesh, in_specs=in_specs, out_specs=out_specs, check_vma=False)
```
